128 devices in a mesh: dp: 2 (over core), expert: 64 (over y, x, z).
Axes of the slice: x: 4, y: 4, z: 4, core: 2. Of those that a mesh axis runs over, the one named last changes fastest.
Arguments:
- tokens: bfloat16 [16384, 2048], P(('dp', 'expert')), may hold values from -6 to 6
- cotangent: bfloat16 [16384, 2048], P(('dp', 'expert')), may hold values from -6 to 6
- routes: int32 [16384, 2], P(('dp', 'expert')), may hold values from 0 to 15, all different within a row; in each aligned block of 128 rows (0 to 127, 128 to 255, ...) at most 24 rows name the same one
- gates: float32 [16384, 2], P(('dp', 'expert')), may hold values from 0.1 to 1
- capacity: int32 [16], replicated, may hold values from 13 to 24, as said below
- layout: int32 [64], replicated, may hold values from 0 to 63, each once
- partner: int32 [64], replicated, may hold values from 0 to 63, as said below
- w_in: float32 [64, 2048, 256], P('expert'), may hold values from -0.125 to 0.125
- w_out: float32 [64, 256, 2048], P('expert'), may hold values from -0.1875 to 0.1875
- m_in: bfloat16 [64, 2048, 256], P('expert'), may hold values from -5 to 5
- v_in: bfloat16 [64, 2048, 256], P('expert'), may hold values from 0.099609375 to 4
- m_out: bfloat16 [64, 256, 2048], P('expert'), may hold values from -5 to 5
- v_out: bfloat16 [64, 256, 2048], P('expert'), may hold values from 0.099609375 to 4
Outputs:
- mixed: bfloat16 [16384, 2048], P(('dp', 'expert'))
- token_grad: bfloat16 [16384, 2048], P(('dp', 'expert'))
- new_w_in: float32 [64, 2048, 256], P('expert')
- new_w_out: float32 [64, 256, 2048], P('expert')
- new_m_in: bfloat16 [64, 2048, 256], P('expert')
- new_v_in: bfloat16 [64, 2048, 256], P('expert')
- new_m_out: bfloat16 [64, 256, 2048], P('expert')
- new_v_out: bfloat16 [64, 256, 2048], P('expert')
The draws below stay inside these ranges and needn't reach their ends.
Inputs may be any that keep to these rules, and one draw needn't show every extreme that they name: `routes`: in the rows of one device no expert is named by more than 24 pairs, a bound that some block reaches; each token names 2 different experts. `capacity`: some expert has exactly 24 and some other exactly that minimum. `layout`: A permutation. partner[d] is d or the index half the expert axis away, and partner[partner[d]] = d; both kinds occur.
All inputs are finite; a program needn't handle non-finite values.
Results may differ from the reference program's by a relative error of at most 0.0079.
Values may be sent and summed in bfloat16 or wider, within the bound.
A program may use at most 128 MiB of HBM per device.

```python
import math
import jax
import jax.numpy as jnp
import numpy as np
from jax import lax

D = 2048
SLICE = 256
GROUP = 4
HIDDEN_UNITS = 1024
TOPK = 2
TOK_DEV = 128
EXPERTS = 16
CAP = 24
TOKENS = 16384
N_DP = 2
N_EXPERT = 64


def draw_capacity(key, part):
    key_a, key_b, key_c = jax.random.split(key, 3)
    caps = jax.random.randint(key_a, (EXPERTS,), CAP // 2 + 1, CAP + 1)
    first = jax.random.randint(key_b, (), 0, EXPERTS)
    other = (first + jax.random.randint(key_c, (), 1, EXPERTS)) % EXPERTS
    index = jnp.arange(EXPERTS)
    caps = jnp.where(index == first, CAP, caps)
    caps = jnp.where(index == other, CAP // 2 + 1, caps)
    return caps.astype(jnp.int32)


def draw_partner(key, part):
    half = N_EXPERT // 2
    flags = jax.random.randint(key, (half,), 0, 2)
    flags = flags.at[0].set(1).at[1].set(0)
    full = jnp.concatenate([flags, flags])
    index = jnp.arange(N_EXPERT)
    across = jnp.where(index < half, index + half, index - half)
    return jnp.where(full == 1, across, index).astype(jnp.int32)


def block_scale(key, extent, cuts, least, top_value):
    gain, own = 1.0, jax.random.fold_in(key, 6)
    for dim, shards_of in cuts:
        steps = jnp.exp(jax.random.uniform(jax.random.fold_in(own, dim), (shards_of,), jnp.float32, least / len(cuts), top_value / len(cuts)))
        gain = gain * jnp.repeat(steps, extent[dim] // shards_of).reshape([-1 if axis == dim else 1 for axis in range(len(extent))])
    return gain


def assign_block(rng, own, number, rows, number_of, top, most, skew):
    order = jax.random.permutation(rng, number_of)
    packed, common = load_shares(number_of, rows * top, most, skew, True), load_shares(number_of, rows * top, most, skew, False)
    places = jnp.arange(number_of)

    def named(lengths, offset_by):
        used = int((lengths > 0).sum())
        fixed = max(1, used // 4)
        passed = fixed + (places - fixed + offset_by * (used - fixed)) % max(1, number_of - fixed)
        return jnp.zeros((number_of,), jnp.int32).at[order[jnp.where(places < fixed, places, passed)]].set(jnp.asarray(lengths, jnp.int32))

    lengths = jnp.where(number % 4 == 0, named(packed, number // 4), named(common, number - number // 4 - 1))
    mixed = jax.random.permutation(jax.random.fold_in(own, 3), number_of)
    giver, sink = mixed[0:number_of // 2 * 2:2], mixed[1:number_of // 2 * 2:2]
    room = jnp.minimum(lengths[giver] - 1, most - lengths[sink]) // 2
    room = jnp.where((giver == order[0]) | (sink == order[0]) | (lengths[sink] == 0), 0, jnp.maximum(room, 0))
    passed = jax.random.randint(jax.random.fold_in(own, 4), (number_of // 2,), 0, 1 << 20) % (room + 1)
    lengths = lengths.at[giver].add(-passed).at[sink].add(passed)
    items = jnp.searchsorted(jnp.cumsum(lengths), jnp.arange(rows * top), side="right").astype(jnp.int32)
    listing = items.reshape(top, rows).T
    listing = listing[jax.random.permutation(jax.random.fold_in(own, 1), rows)]
    offset_by = jax.random.randint(jax.random.fold_in(own, 2), (rows, 1), 0, top)
    return jnp.take_along_axis(listing, (jnp.arange(top)[None, :] + offset_by) % top, axis=1)


def load_shares(number_of, total, bound, slope, full):
    portions = [(1 << 20) // math.isqrt(grade ** slope) + 1 for grade in range(1, number_of + 1)]
    largest = bound if full else min(bound, max(-(-total // number_of), total * portions[0] // sum(portions)))
    least = 1 if total - largest >= number_of - 1 else 0
    holding, rest = [largest] + [least] * (number_of - 1), total - largest - least * (number_of - 1)
    while rest > 0:
        movable = [i for i in range(1, number_of) if holding[i] < largest] or [i for i in range(1, number_of) if holding[i] < bound]
        mass, remaining = sum([portions[i] for i in movable]), rest
        for i in movable:
            addition = min(bound - holding[i], max(1, remaining * portions[i] // mass), rest)
            holding[i] = holding[i] + addition
            rest = rest - addition
    return np.array(holding)


def centred(stream_key, dims, width, reach, cuts=(), kind=jnp.bfloat16):
    drawn = jax.random.normal(stream_key, dims, jnp.float32) * width
    if len(cuts) > 0:
        drawn = block_scale(stream_key, dims, cuts, -0.22, 0.18) * drawn
    return jnp.clip(drawn, min=-reach, max=reach).astype(kind)


def setup_inputs(seed: int = 0) -> dict:
    seeds = jax.random.split(jax.random.key(seed), 14)
    tokens = centred(seeds[0], (TOKENS, D), 1.0, 6.0, ((0, 128),))
    cotangent = centred(seeds[1], (TOKENS, D), 1.0, 6.0, ((0, 128),))
    routes_keys = jax.random.split(jax.random.fold_in(seeds[2], 1), TOKENS // TOK_DEV)
    routes_turns = jax.random.permutation(jax.random.fold_in(seeds[2], 3), TOKENS // TOK_DEV)
    routes = jax.vmap(lambda own, number: assign_block(jax.random.fold_in(seeds[2], 2), own, number, TOK_DEV, EXPERTS, TOPK, CAP, 2))(routes_keys, routes_turns).reshape((TOKENS, TOPK))
    gates = jnp.clip(0.1 + 0.9 * jax.random.uniform(seeds[3], (TOKENS, TOPK), jnp.float32) ** block_scale(seeds[3], (TOKENS, TOPK), ((0, 128),), -0.2, 0.2), 0.1, 1.0)
    capacity = draw_capacity(jax.random.fold_in(seeds[13], 71), 0)
    layout = jax.random.permutation(seeds[5], N_EXPERT).astype(jnp.int32)
    partner = draw_partner(jax.random.fold_in(seeds[13], 71), 0)
    w_in = centred(seeds[7], (N_EXPERT, D, SLICE), D ** -0.5, 0.125, ((0, 64),), jnp.float32)
    w_out = centred(seeds[8], (N_EXPERT, SLICE, D), HIDDEN_UNITS ** -0.5, 0.1875, ((0, 64),), jnp.float32)
    m_in = centred(seeds[9], (N_EXPERT, D, SLICE), 1.0, 5.0, ((0, 64),))
    v_in = jnp.clip(jnp.exp(math.log(4.0) - 3.6927934 * jax.random.uniform(seeds[10], (N_EXPERT, D, SLICE), jnp.float32) ** block_scale(seeds[10], (N_EXPERT, D, SLICE), ((0, 64),), -0.2, 0.2)), 0.099609375, 4.0).astype(jnp.bfloat16)
    m_out = centred(seeds[11], (N_EXPERT, SLICE, D), 1.0, 5.0, ((0, 64),))
    v_out = jnp.clip(jnp.exp(math.log(4.0) - 3.6927934 * jax.random.uniform(seeds[12], (N_EXPERT, SLICE, D), jnp.float32) ** block_scale(seeds[12], (N_EXPERT, SLICE, D), ((0, 64),), -0.2, 0.2)), 0.099609375, 4.0).astype(jnp.bfloat16)
    return {"tokens": tokens, "cotangent": cotangent, "routes": routes, "gates": gates, "capacity": capacity, "layout": layout, "partner": partner, "w_in": w_in, "w_out": w_out, "m_in": m_in, "v_in": v_in, "m_out": m_out, "v_out": v_out}


def gelu_tanh(value):
    return jax.nn.gelu(value, approximate=True)

def adamw(weight, first, second, grad):
    first_f = 0.9 * first.astype(jnp.float32) + 0.1 * grad
    second_f = 0.999 * second.astype(jnp.float32) + 0.001 * grad * grad
    corrected = first_f / (1.0 - 0.9 ** 10) / (jnp.sqrt(second_f / (1.0 - 0.999 ** 10)) + 1e-08)
    updated = weight - 0.01 * (corrected + 0.1 * weight)
    return (updated, first_f.astype(jnp.bfloat16), second_f.astype(jnp.bfloat16))

def fdot(left, right):
    return jnp.dot(left.astype(jnp.float32), right.astype(jnp.float32), preferred_element_type=jnp.float32)

def reference(tokens, cotangent, routes, gates, capacity, layout, partner, w_in, w_out, m_in, v_in, m_out, v_out):
    sources = N_DP * N_EXPERT
    pairs = TOK_DEV * TOPK

    def slots_of(block):
        onehot = (block[:, None] == jnp.arange(EXPERTS, dtype=jnp.int32)[None, :]).astype(jnp.int32)
        position = lax.optimization_barrier(jnp.sum((jnp.cumsum(onehot, 0) - 1) * onehot, 1))
        limit = lax.optimization_barrier(jnp.sum(onehot * capacity[None, :], 1))
        return jnp.where(position < limit, block * CAP + position, EXPERTS * CAP).astype(jnp.int32)
    slot = jax.vmap(slots_of)(routes.reshape(sources, pairs))
    x_rows = jnp.repeat(tokens, TOPK, axis=0).reshape(sources, pairs, D)
    scaled = (gates.reshape(-1)[:, None] * jnp.repeat(cotangent, TOPK, axis=0).astype(jnp.float32)).astype(jnp.bfloat16)
    scaled = scaled.reshape(sources, pairs, D)

    def build(rows, places):
        filled = jnp.zeros((EXPERTS * CAP + 1, D), jnp.bfloat16).at[places].set(rows)
        return filled[:-1].reshape(EXPERTS, CAP, D)
    x_buf = jax.vmap(build)(x_rows, slot)
    g_buf = jax.vmap(build)(scaled, slot)
    inverse = jnp.zeros((N_EXPERT,), jnp.int32).at[layout].set(jnp.arange(N_EXPERT, dtype=jnp.int32))

    def per_expert(expert):
        rows = jnp.take(x_buf, expert, axis=1).reshape(sources * CAP, D)
        grows = jnp.take(g_buf, expert, axis=1).reshape(sources * CAP, D)
        out_sum = jnp.zeros((sources * CAP, D), jnp.float32)
        dx_sum = jnp.zeros((sources * CAP, D), jnp.float32)
        states = []
        for piece in range(GROUP):
            holder = inverse[expert * GROUP + piece]
            weight_in = jnp.take(w_in, holder, axis=0)
            weight_out = jnp.take(w_out, holder, axis=0)
            wb_in = weight_in.astype(jnp.bfloat16)
            wb_out = weight_out.astype(jnp.bfloat16)
            pre = fdot(rows, wb_in)
            hidden, pull = jax.vjp(gelu_tanh, pre)
            hidden = hidden.astype(jnp.bfloat16)
            part = fdot(hidden, wb_out).astype(jnp.bfloat16)
            dhid = fdot(grows, wb_out.T)
            dpre = pull(dhid)[0].astype(jnp.bfloat16)
            xpart = fdot(dpre, wb_in.T).astype(jnp.bfloat16)
            grad_in = fdot(rows.T, dpre)
            grad_out = fdot(hidden.T, grows)
            out_sum = out_sum + part.astype(jnp.float32)
            dx_sum = dx_sum + xpart.astype(jnp.float32)
            new_in = adamw(weight_in, jnp.take(m_in, holder, axis=0), jnp.take(v_in, holder, axis=0), grad_in)
            new_out = adamw(weight_out, jnp.take(m_out, holder, axis=0), jnp.take(v_out, holder, axis=0), grad_out)
            states.append(new_in + new_out)
        stacked = tuple((jnp.stack([state[index] for state in states]) for index in range(6)))
        return (out_sum, dx_sum, stacked)
    out_sum, dx_sum, stacked = lax.map(per_expert, jnp.arange(EXPERTS, dtype=jnp.int32))

    def regroup(values):
        values = values.reshape(EXPERTS, sources, CAP, D).transpose(1, 0, 2, 3).reshape(sources, EXPERTS * CAP, D)
        values = jnp.concatenate([values, jnp.zeros((sources, 1, D), jnp.float32)], axis=1)
        return jax.vmap(lambda table, places: jnp.take(table, places, axis=0))(values, slot)
    outs = regroup(out_sum).reshape(sources, TOK_DEV, TOPK, D)
    grads = regroup(dx_sum).reshape(sources, TOK_DEV, TOPK, D)
    mixed = lax.optimization_barrier(jnp.sum(outs * gates.reshape(sources, TOK_DEV, TOPK, 1), axis=2)).reshape(TOKENS, D).astype(jnp.bfloat16)
    token_grad = lax.optimization_barrier(jnp.sum(grads, axis=2)).reshape(TOKENS, D).astype(jnp.bfloat16)
    target = jnp.take(layout, partner, axis=0).astype(jnp.int32)
    shapes = [(D, SLICE), (D, SLICE), (D, SLICE), (SLICE, D), (SLICE, D), (SLICE, D)]
    moved = [jnp.take(stacked[index].reshape((N_EXPERT,) + shapes[index]), target, axis=0) for index in range(6)]
    return (mixed, token_grad, moved[0], moved[3], moved[1], moved[2], moved[4], moved[5])
```

```python
import jax
import jax.numpy as jnp
from jax import lax
from jax.sharding import PartitionSpec as P

GROUP = 4


def relay(block, step):
    ndp = lax.axis_size("dp")
    nexp = lax.axis_size("expert")
    route = []
    for d in range(ndp):
        sign = 1 if d % 2 == 0 else -1
        for e in range(nexp):
            route.append((d * nexp + e, d * nexp + (e + sign * step) % nexp))
    return lax.ppermute(block, ("dp", "expert"), route)


def migrate(blocks):
    ndp = lax.axis_size("dp")
    step = lax.axis_size("expert") // 4
    here = lax.axis_index("dp")
    halves = tuple(
        lax.dynamic_slice_in_dim(b, here * (b.shape[0] // ndp), b.shape[0] // ndp, 0)
        for b in blocks
    )
    moved = relay(relay(halves, step), step)
    return tuple(lax.all_gather(m, "dp", axis=0, tiled=True) for m in moved)


def gelu_tanh(value):
    return jax.nn.gelu(value, approximate=True)


def adamw(weight, first, second, grad):
    first_f = 0.9 * first.astype(jnp.float32) + 0.1 * grad
    second_f = 0.999 * second.astype(jnp.float32) + 0.001 * grad * grad
    corrected = first_f / (1.0 - 0.9**10) / (jnp.sqrt(second_f / (1.0 - 0.999**10)) + 1e-08)
    updated = weight - 0.01 * (corrected + 0.1 * weight)
    return (updated, first_f.astype(jnp.bfloat16), second_f.astype(jnp.bfloat16))


def local(
    tokens,
    cotangent,
    routes,
    gates,
    capacity,
    layout,
    partner,
    w_in,
    w_out,
    m_in,
    v_in,
    m_out,
    v_out,
):
    width = tokens.shape[1]
    count = tokens.shape[0]
    topk = routes.shape[1]
    experts = capacity.shape[0]
    slots = 3 * count * topk // (2 * experts)
    nexp = lax.axis_size("expert")
    here = lax.axis_index("expert")
    moved = jnp.take(partner, here) != here
    flat_routes = routes.reshape(-1)
    onehot = (flat_routes[:, None] == jnp.arange(experts, dtype=jnp.int32)[None, :]).astype(
        jnp.int32
    )
    position = jnp.sum((jnp.cumsum(onehot, 0) - 1) * onehot, 1)
    limit = jnp.sum(onehot * capacity[None, :], 1)
    slot = jnp.where(position < limit, flat_routes * slots + position, experts * slots)
    x_rows = jnp.repeat(tokens, topk, axis=0)
    scaled = (
        gates.reshape(-1)[:, None] * jnp.repeat(cotangent, topk, axis=0).astype(jnp.float32)
    ).astype(jnp.bfloat16)

    def build(rows):
        filled = jnp.zeros((experts * slots + 1, width), jnp.bfloat16).at[slot].set(rows)
        return filled[:-1].reshape(experts, slots, width)

    x_buf = build(x_rows)
    g_buf = build(scaled)
    weight_in, weight_out = (w_in[0], w_out[0])
    first_in, second_in, first_out, second_out = (m_in[0], v_in[0], m_out[0], v_out[0])
    held = jnp.take(layout, partner, axis=0)
    other = migrate(
        (
            weight_in.astype(jnp.bfloat16),
            weight_out.astype(jnp.bfloat16),
            first_in,
            second_in,
            first_out,
            second_out,
        )
    )
    other_w = (other[0].astype(weight_in.dtype), other[1].astype(weight_out.dtype))
    other_m = other[2:]
    weight_in = jnp.where(moved, other_w[0], weight_in)
    weight_out = jnp.where(moved, other_w[1], weight_out)
    first_in = jnp.where(moved, other_m[0], first_in)
    second_in = jnp.where(moved, other_m[1], second_in)
    first_out = jnp.where(moved, other_m[2], first_out)
    second_out = jnp.where(moved, other_m[3], second_out)
    target_expert = held // GROUP
    send_x = jnp.take(x_buf, target_expert, axis=0)
    send_g = jnp.take(g_buf, target_expert, axis=0)
    recv_x, recv_g = (
        lax.all_to_all(send_x, "expert", split_axis=0, concat_axis=0, tiled=True),
        lax.all_to_all(send_g, "expert", split_axis=0, concat_axis=0, tiled=True),
    )
    rows = recv_x.reshape(-1, width)
    grows = recv_g.reshape(-1, width)
    wb_in = weight_in.astype(jnp.bfloat16)
    wb_out = weight_out.astype(jnp.bfloat16)
    pre = jnp.dot(rows, wb_in, preferred_element_type=jnp.float32)
    hidden, pull = jax.vjp(gelu_tanh, pre)
    hidden = hidden.astype(jnp.bfloat16)
    part = jnp.dot(hidden, wb_out, preferred_element_type=jnp.float32).astype(jnp.bfloat16)
    dhid = lax.dot_general(
        grows, wb_out, (((1,), (1,)), ((), ())), preferred_element_type=jnp.float32
    )
    dpre = pull(dhid)[0].astype(jnp.bfloat16)
    xpart = lax.dot_general(
        dpre, wb_in, (((1,), (1,)), ((), ())), preferred_element_type=jnp.float32
    ).astype(jnp.bfloat16)
    grad_in = lax.dot_general(
        rows, dpre, (((0,), (0,)), ((), ())), preferred_element_type=jnp.float32
    )
    grad_out = lax.dot_general(
        hidden, grows, (((0,), (0,)), ((), ())), preferred_element_type=jnp.float32
    )
    back_part, back_dx = (
        lax.all_to_all(
            part.reshape(nexp, slots, width), "expert", split_axis=0, concat_axis=0, tiled=True
        ),
        lax.all_to_all(
            xpart.reshape(nexp, slots, width), "expert", split_axis=0, concat_axis=0, tiled=True
        ),
    )
    grad_in, grad_out = lax.psum((grad_in, grad_out), "dp")
    new_w_in, new_m_in, new_v_in = adamw(weight_in, first_in, second_in, grad_in)
    new_w_out, new_m_out, new_v_out = adamw(weight_out, first_out, second_out, grad_out)
    owners = (target_expert[:, None] == jnp.arange(experts, dtype=jnp.int32)[None, :]).astype(
        jnp.bfloat16
    )
    out_sum = jnp.einsum("je,jcd->ecd", owners, back_part, preferred_element_type=jnp.float32)
    dx_sum = jnp.einsum("je,jcd->ecd", owners, back_dx, preferred_element_type=jnp.float32)
    blank = jnp.zeros((1, width), jnp.float32)
    out_vals = jnp.take(jnp.concatenate([out_sum.reshape(-1, width), blank]), slot, axis=0)
    dx_vals = jnp.take(jnp.concatenate([dx_sum.reshape(-1, width), blank]), slot, axis=0)
    mixed = jnp.sum(out_vals.reshape(count, topk, width) * gates[:, :, None], axis=1).astype(
        jnp.bfloat16
    )
    token_grad = jnp.sum(dx_vals.reshape(count, topk, width), axis=1).astype(jnp.bfloat16)
    return (
        mixed,
        token_grad,
        new_w_in[None],
        new_w_out[None],
        new_m_in[None],
        new_v_in[None],
        new_m_out[None],
        new_v_out[None],
    )


def solution(mesh):
    in_specs = (
        P(("dp", "expert"), None),
        P(("dp", "expert"), None),
        P(("dp", "expert"), None),
        P(("dp", "expert"), None),
        P(),
        P(),
        P(),
        P("expert", None, None),
        P("expert", None, None),
        P("expert", None, None),
        P("expert", None, None),
        P("expert", None, None),
        P("expert", None, None),
    )
    out_specs = (
        P(("dp", "expert"), None),
        P(("dp", "expert"), None),
        P("expert", None, None),
        P("expert", None, None),
        P("expert", None, None),
        P("expert", None, None),
        P("expert", None, None),
        P("expert", None, None),
    )
    return jax.shard_map(local, mesh=mesh, in_specs=in_specs, out_specs=out_specs, check_vma=False)
```

```python
import jax
import jax.numpy as jnp
from jax import lax
from jax.sharding import PartitionSpec as P

GROUP = 4


def relay(block, step):
    ndp = lax.axis_size("dp")
    nexp = lax.axis_size("expert")
    route = []
    for d in range(ndp):
        sign = 1 if d % 2 == 0 else -1
        for e in range(nexp):
            route.append((d * nexp + e, d * nexp + (e + sign * step) % nexp))
    return lax.ppermute(block, ("dp", "expert"), route)


def migrate(blocks):
    ndp = lax.axis_size("dp")
    step = lax.axis_size("expert") // 4
    here = lax.axis_index("dp")
    halves = tuple(
        lax.dynamic_slice_in_dim(b, here * (b.shape[0] // ndp), b.shape[0] // ndp, 0)
        for b in blocks
    )
    moved = relay(relay(halves, step), step)
    return tuple(lax.all_gather(m, "dp", axis=0, tiled=True) for m in moved)


def gelu_tanh(value):
    return jax.nn.gelu(value, approximate=True)


def adamw(weight, first, second, grad):
    first_f = 0.9 * first.astype(jnp.float32) + 0.1 * grad
    second_f = 0.999 * second.astype(jnp.float32) + 0.001 * grad * grad
    corrected = first_f / (1.0 - 0.9**10) / (jnp.sqrt(second_f / (1.0 - 0.999**10)) + 1e-08)
    updated = weight - 0.01 * (corrected + 0.1 * weight)
    return (updated, first_f.astype(jnp.bfloat16), second_f.astype(jnp.bfloat16))


def local(
    tokens,
    cotangent,
    routes,
    gates,
    capacity,
    layout,
    partner,
    w_in,
    w_out,
    m_in,
    v_in,
    m_out,
    v_out,
):
    width = tokens.shape[1]
    count = tokens.shape[0]
    topk = routes.shape[1]
    experts = capacity.shape[0]
    slots = 3 * count * topk // (2 * experts)
    nexp = lax.axis_size("expert")
    here = lax.axis_index("expert")
    moved = jnp.take(partner, here) != here
    flat_routes = routes.reshape(-1)
    onehot = (flat_routes[:, None] == jnp.arange(experts, dtype=jnp.int32)[None, :]).astype(
        jnp.int32
    )
    position = jnp.sum((jnp.cumsum(onehot, 0) - 1) * onehot, 1)
    limit = jnp.sum(onehot * capacity[None, :], 1)
    kept = position < limit
    npairs = count * topk
    slot = jnp.where(kept, flat_routes * slots + position, experts * slots)
    pair_of = (
        jnp.full((experts * slots + 1,), npairs, jnp.int32)
        .at[slot]
        .set(jnp.arange(npairs, dtype=jnp.int32))[:-1]
        .reshape(experts, slots)
    )
    held = jnp.take(layout, partner, axis=0)
    target_expert = held // GROUP
    send_pair = jnp.take(pair_of, target_expert, axis=0)
    send_tok = jnp.where(send_pair < npairs, send_pair // topk, count)
    gate_of = jnp.concatenate([gates.reshape(-1), jnp.zeros((1,), gates.dtype)])
    blank = jnp.zeros((1, width), tokens.dtype)
    send_x = jnp.take(jnp.concatenate([tokens, blank]), send_tok, axis=0)
    send_g = (
        jnp.take(gate_of, send_pair)[:, :, None]
        * jnp.take(jnp.concatenate([cotangent, blank]), send_tok, axis=0).astype(jnp.float32)
    ).astype(jnp.bfloat16)
    weight_in, weight_out = (w_in[0], w_out[0])
    first_in, second_in, first_out, second_out = (m_in[0], v_in[0], m_out[0], v_out[0])
    other = migrate(
        (
            weight_in.astype(jnp.bfloat16),
            weight_out.astype(jnp.bfloat16),
            first_in,
            second_in,
            first_out,
            second_out,
        )
    )
    send_x, send_g, other = lax.optimization_barrier((send_x, send_g, other))
    other_w = (other[0].astype(weight_in.dtype), other[1].astype(weight_out.dtype))
    other_m = other[2:]
    weight_in = jnp.where(moved, other_w[0], weight_in)
    weight_out = jnp.where(moved, other_w[1], weight_out)
    first_in = jnp.where(moved, other_m[0], first_in)
    second_in = jnp.where(moved, other_m[1], second_in)
    first_out = jnp.where(moved, other_m[2], first_out)
    second_out = jnp.where(moved, other_m[3], second_out)
    recv_x, recv_g = (
        lax.all_to_all(send_x, "expert", split_axis=0, concat_axis=0, tiled=True),
        lax.all_to_all(send_g, "expert", split_axis=0, concat_axis=0, tiled=True),
    )
    rows = recv_x.reshape(-1, width)
    grows = recv_g.reshape(-1, width)
    wb_in = weight_in.astype(jnp.bfloat16)
    wb_out = weight_out.astype(jnp.bfloat16)
    pre = jnp.dot(rows, wb_in, preferred_element_type=jnp.float32)
    hidden, pull = jax.vjp(gelu_tanh, pre)
    hidden = hidden.astype(jnp.bfloat16)
    part = jnp.dot(hidden, wb_out, preferred_element_type=jnp.float32).astype(jnp.bfloat16)
    dhid = lax.dot_general(
        grows, wb_out, (((1,), (1,)), ((), ())), preferred_element_type=jnp.float32
    )
    dpre = pull(dhid)[0].astype(jnp.bfloat16)
    xpart = lax.dot_general(
        dpre, wb_in, (((1,), (1,)), ((), ())), preferred_element_type=jnp.float32
    ).astype(jnp.bfloat16)
    grad_in = lax.dot_general(
        rows, dpre, (((0,), (0,)), ((), ())), preferred_element_type=jnp.float32
    )
    grad_out = lax.dot_general(
        hidden, grows, (((0,), (0,)), ((), ())), preferred_element_type=jnp.float32
    )
    back_part, back_dx = (
        lax.all_to_all(
            part.reshape(nexp, slots, width), "expert", split_axis=0, concat_axis=0, tiled=True
        ),
        lax.all_to_all(
            xpart.reshape(nexp, slots, width), "expert", split_axis=0, concat_axis=0, tiled=True
        ),
    )
    grad_in, grad_out = lax.psum((grad_in, grad_out), "dp")
    new_w_in, new_m_in, new_v_in = adamw(weight_in, first_in, second_in, grad_in)
    new_w_out, new_m_out, new_v_out = adamw(weight_out, first_out, second_out, grad_out)
    holder_of = jnp.zeros((nexp,), jnp.int32).at[held].set(jnp.arange(nexp, dtype=jnp.int32))
    shard_ids = flat_routes[:, None] * GROUP + jnp.arange(GROUP, dtype=jnp.int32)[None, :]
    back_row = jnp.where(
        kept[:, None], jnp.take(holder_of, shard_ids) * slots + position[:, None], nexp * slots
    )
    zero = jnp.zeros((1, width), jnp.bfloat16)

    def gather_sum(back):
        table = jnp.concatenate([back.reshape(-1, width), zero])
        return jnp.sum(jnp.take(table, back_row, axis=0).astype(jnp.float32), axis=1)

    out_vals = gather_sum(back_part)
    dx_vals = gather_sum(back_dx)
    mixed = jnp.sum(out_vals.reshape(count, topk, width) * gates[:, :, None], axis=1).astype(
        jnp.bfloat16
    )
    token_grad = jnp.sum(dx_vals.reshape(count, topk, width), axis=1).astype(jnp.bfloat16)
    return (
        mixed,
        token_grad,
        new_w_in[None],
        new_w_out[None],
        new_m_in[None],
        new_v_in[None],
        new_m_out[None],
        new_v_out[None],
    )


def solution(mesh):
    in_specs = (
        P(("dp", "expert"), None),
        P(("dp", "expert"), None),
        P(("dp", "expert"), None),
        P(("dp", "expert"), None),
        P(),
        P(),
        P(),
        P("expert", None, None),
        P("expert", None, None),
        P("expert", None, None),
        P("expert", None, None),
        P("expert", None, None),
        P("expert", None, None),
    )
    out_specs = (
        P(("dp", "expert"), None),
        P(("dp", "expert"), None),
        P("expert", None, None),
        P("expert", None, None),
        P("expert", None, None),
        P("expert", None, None),
        P("expert", None, None),
        P("expert", None, None),
    )
    return jax.shard_map(local, mesh=mesh, in_specs=in_specs, out_specs=out_specs, check_vma=False)
```

```python
import jax
import jax.numpy as jnp
from jax import lax
from jax.sharding import PartitionSpec as P

GROUP = 4


def relay(block, step):
    ndp = lax.axis_size("dp")
    nexp = lax.axis_size("expert")
    route = []
    for d in range(ndp):
        sign = 1 if d % 2 == 0 else -1
        for e in range(nexp):
            route.append((d * nexp + e, d * nexp + (e + sign * step) % nexp))
    return lax.ppermute(block, ("dp", "expert"), route)


def migrate(blocks):
    ndp = lax.axis_size("dp")
    step = lax.axis_size("expert") // 4
    here = lax.axis_index("dp")
    halves = tuple(
        lax.dynamic_slice_in_dim(b, here * (b.shape[0] // ndp), b.shape[0] // ndp, 0)
        for b in blocks
    )
    moved = relay(relay(halves, step), step)
    return tuple(lax.all_gather(m, "dp", axis=0, tiled=True) for m in moved)


def gelu_tanh(value):
    return jax.nn.gelu(value, approximate=True)


def adamw(weight, first, second, grad):
    first_f = 0.9 * first.astype(jnp.float32) + 0.1 * grad
    second_f = 0.999 * second.astype(jnp.float32) + 0.001 * grad * grad
    corrected = first_f / (1.0 - 0.9**10) / (jnp.sqrt(second_f / (1.0 - 0.999**10)) + 1e-08)
    updated = weight - 0.01 * (corrected + 0.1 * weight)
    return (updated, first_f.astype(jnp.bfloat16), second_f.astype(jnp.bfloat16))


def local(
    tokens,
    cotangent,
    routes,
    gates,
    capacity,
    layout,
    partner,
    w_in,
    w_out,
    m_in,
    v_in,
    m_out,
    v_out,
):
    width = tokens.shape[1]
    count = tokens.shape[0]
    topk = routes.shape[1]
    experts = capacity.shape[0]
    slots = 3 * count * topk // (2 * experts)
    nexp = lax.axis_size("expert")
    here = lax.axis_index("expert")
    moved = jnp.take(partner, here) != here
    flat_routes = routes.reshape(-1)
    onehot = (flat_routes[:, None] == jnp.arange(experts, dtype=jnp.int32)[None, :]).astype(
        jnp.int32
    )
    position = jnp.sum((jnp.cumsum(onehot, 0) - 1) * onehot, 1)
    limit = jnp.sum(onehot * capacity[None, :], 1)
    kept = position < limit
    npairs = count * topk
    slot = jnp.where(kept, flat_routes * slots + position, experts * slots)
    pair_of = (
        jnp.full((experts * slots + 1,), npairs, jnp.int32)
        .at[slot]
        .set(jnp.arange(npairs, dtype=jnp.int32))[:-1]
        .reshape(experts, slots)
    )
    held = jnp.take(layout, partner, axis=0)
    target_expert = held // GROUP
    send_pair = jnp.take(pair_of, target_expert, axis=0)
    send_tok = jnp.where(send_pair < npairs, send_pair // topk, count)
    gate_of = jnp.concatenate([gates.reshape(-1), jnp.zeros((1,), gates.dtype)])
    pick = (send_tok[:, :, None] == jnp.arange(count, dtype=jnp.int32)[None, None, :]).astype(
        jnp.bfloat16
    )
    pick = pick.reshape(nexp * slots, count)
    send_x = (
        jnp.dot(pick, tokens, preferred_element_type=jnp.float32)
        .astype(jnp.bfloat16)
        .reshape(nexp, slots, width)
    )
    send_g = (
        jnp.take(gate_of, send_pair)[:, :, None]
        * jnp.dot(pick, cotangent, preferred_element_type=jnp.float32)
        .astype(jnp.bfloat16)
        .astype(jnp.float32)
        .reshape(nexp, slots, width)
    ).astype(jnp.bfloat16)
    weight_in, weight_out = (w_in[0], w_out[0])
    first_in, second_in, first_out, second_out = (m_in[0], v_in[0], m_out[0], v_out[0])
    other = migrate(
        (
            weight_in.astype(jnp.bfloat16),
            weight_out.astype(jnp.bfloat16),
            first_in,
            second_in,
            first_out,
            second_out,
        )
    )
    send_x, send_g, other = lax.optimization_barrier((send_x, send_g, other))
    other_w = (other[0].astype(weight_in.dtype), other[1].astype(weight_out.dtype))
    other_m = other[2:]
    weight_in = jnp.where(moved, other_w[0], weight_in)
    weight_out = jnp.where(moved, other_w[1], weight_out)
    first_in = jnp.where(moved, other_m[0], first_in)
    second_in = jnp.where(moved, other_m[1], second_in)
    first_out = jnp.where(moved, other_m[2], first_out)
    second_out = jnp.where(moved, other_m[3], second_out)
    recv_x, recv_g = (
        lax.all_to_all(send_x, "expert", split_axis=0, concat_axis=0, tiled=True),
        lax.all_to_all(send_g, "expert", split_axis=0, concat_axis=0, tiled=True),
    )
    rows = recv_x.reshape(-1, width)
    grows = recv_g.reshape(-1, width)
    wb_in = weight_in.astype(jnp.bfloat16)
    wb_out = weight_out.astype(jnp.bfloat16)
    pre = jnp.dot(rows, wb_in, preferred_element_type=jnp.float32)
    hidden, pull = jax.vjp(gelu_tanh, pre)
    hidden = hidden.astype(jnp.bfloat16)
    part = jnp.dot(hidden, wb_out, preferred_element_type=jnp.float32).astype(jnp.bfloat16)
    dhid = lax.dot_general(
        grows, wb_out, (((1,), (1,)), ((), ())), preferred_element_type=jnp.float32
    )
    dpre = pull(dhid)[0].astype(jnp.bfloat16)
    xpart = lax.dot_general(
        dpre, wb_in, (((1,), (1,)), ((), ())), preferred_element_type=jnp.float32
    ).astype(jnp.bfloat16)
    grad_in = lax.dot_general(
        rows, dpre, (((0,), (0,)), ((), ())), preferred_element_type=jnp.float32
    )
    grad_out = lax.dot_general(
        hidden, grows, (((0,), (0,)), ((), ())), preferred_element_type=jnp.float32
    )
    back_part, back_dx = (
        lax.all_to_all(
            part.reshape(nexp, slots, width), "expert", split_axis=0, concat_axis=0, tiled=True
        ),
        lax.all_to_all(
            xpart.reshape(nexp, slots, width), "expert", split_axis=0, concat_axis=0, tiled=True
        ),
    )
    grad_in, grad_out = lax.psum((grad_in, grad_out), "dp")
    new_w_in, new_m_in, new_v_in = adamw(weight_in, first_in, second_in, grad_in)
    new_w_out, new_m_out, new_v_out = adamw(weight_out, first_out, second_out, grad_out)
    row_expert = jnp.repeat(target_expert, slots)
    row_pos = jnp.tile(jnp.arange(slots, dtype=jnp.int32), nexp)
    owns = (
        kept[:, None]
        & (flat_routes[:, None] == row_expert[None, :])
        & (position[:, None] == row_pos[None, :])
    )
    owns_pair = owns.astype(jnp.bfloat16)
    owns_tok = owns.reshape(count, topk, nexp * slots).any(axis=1).astype(jnp.bfloat16)
    out_vals = jnp.dot(
        owns_pair, back_part.reshape(-1, width), preferred_element_type=jnp.float32
    )
    mixed = jnp.sum(out_vals.reshape(count, topk, width) * gates[:, :, None], axis=1).astype(
        jnp.bfloat16
    )
    token_grad = jnp.dot(
        owns_tok, back_dx.reshape(-1, width), preferred_element_type=jnp.float32
    ).astype(jnp.bfloat16)
    return (
        mixed,
        token_grad,
        new_w_in[None],
        new_w_out[None],
        new_m_in[None],
        new_v_in[None],
        new_m_out[None],
        new_v_out[None],
    )


def solution(mesh):
    in_specs = (
        P(("dp", "expert"), None),
        P(("dp", "expert"), None),
        P(("dp", "expert"), None),
        P(("dp", "expert"), None),
        P(),
        P(),
        P(),
        P("expert", None, None),
        P("expert", None, None),
        P("expert", None, None),
        P("expert", None, None),
        P("expert", None, None),
        P("expert", None, None),
    )
    out_specs = (
        P(("dp", "expert"), None),
        P(("dp", "expert"), None),
        P("expert", None, None),
        P("expert", None, None),
        P("expert", None, None),
        P("expert", None, None),
        P("expert", None, None),
        P("expert", None, None),
    )
    return jax.shard_map(local, mesh=mesh, in_specs=in_specs, out_specs=out_specs, check_vma=False)
```

```python
import jax
import jax.numpy as jnp
from jax import lax
from jax.sharding import PartitionSpec as P

GROUP = 4


def relay(block, step):
    ndp = lax.axis_size("dp")
    nexp = lax.axis_size("expert")
    route = []
    for d in range(ndp):
        sign = 1 if d % 2 == 0 else -1
        for e in range(nexp):
            route.append((d * nexp + e, d * nexp + (e + sign * step) % nexp))
    return lax.ppermute(block, ("dp", "expert"), route)


def migrate(blocks):
    ndp = lax.axis_size("dp")
    step = lax.axis_size("expert") // 4
    here = lax.axis_index("dp")
    halves = [
        lax.dynamic_slice_in_dim(b, here * (b.shape[0] // ndp), b.shape[0] // ndp, 0)
        for b in blocks
    ]
    lanes = 128
    packed = jnp.concatenate([h.reshape(-1, lanes) for h in halves], axis=0)
    moved = relay(relay(packed, step), step)
    whole = lax.all_gather(moved, "dp", axis=0, tiled=False)
    out = []
    offset = 0
    for h in halves:
        n = h.size // lanes
        piece = whole[:, offset : offset + n].reshape((ndp * h.shape[0],) + h.shape[1:])
        out.append(piece)
        offset += n
    return tuple(out)


def gelu_tanh(value):
    return jax.nn.gelu(value, approximate=True)


def adamw(weight, first, second, grad):
    first_f = 0.9 * first.astype(jnp.float32) + 0.1 * grad
    second_f = 0.999 * second.astype(jnp.float32) + 0.001 * grad * grad
    corrected = first_f / (1.0 - 0.9**10) / (jnp.sqrt(second_f / (1.0 - 0.999**10)) + 1e-08)
    updated = weight - 0.01 * (corrected + 0.1 * weight)
    return (updated, first_f.astype(jnp.bfloat16), second_f.astype(jnp.bfloat16))


def local(
    tokens,
    cotangent,
    routes,
    gates,
    capacity,
    layout,
    partner,
    w_in,
    w_out,
    m_in,
    v_in,
    m_out,
    v_out,
):
    width = tokens.shape[1]
    count = tokens.shape[0]
    topk = routes.shape[1]
    experts = capacity.shape[0]
    slots = 3 * count * topk // (2 * experts)
    nexp = lax.axis_size("expert")
    here = lax.axis_index("expert")
    moved = jnp.take(partner, here) != here
    flat_routes = routes.reshape(-1)
    onehot = (flat_routes[:, None] == jnp.arange(experts, dtype=jnp.int32)[None, :]).astype(
        jnp.int32
    )
    position = jnp.sum((jnp.cumsum(onehot, 0) - 1) * onehot, 1)
    limit = jnp.sum(onehot * capacity[None, :], 1)
    kept = position < limit
    npairs = count * topk
    slot = jnp.where(kept, flat_routes * slots + position, experts * slots)
    pair_of = (
        jnp.full((experts * slots + 1,), npairs, jnp.int32)
        .at[slot]
        .set(jnp.arange(npairs, dtype=jnp.int32))[:-1]
        .reshape(experts, slots)
    )
    held = jnp.take(layout, partner, axis=0)
    target_expert = held // GROUP
    send_pair = jnp.take(pair_of, target_expert, axis=0)
    send_tok = jnp.where(send_pair < npairs, send_pair // topk, count)
    gate_of = jnp.concatenate([gates.reshape(-1), jnp.zeros((1,), gates.dtype)])
    pick = (send_tok[:, :, None] == jnp.arange(count, dtype=jnp.int32)[None, None, :]).astype(
        jnp.bfloat16
    )
    pick = pick.reshape(nexp * slots, count)
    send_x = (
        jnp.dot(pick, tokens, preferred_element_type=jnp.float32)
        .astype(jnp.bfloat16)
        .reshape(nexp, slots, width)
    )
    send_g = (
        jnp.take(gate_of, send_pair)[:, :, None]
        * jnp.dot(pick, cotangent, preferred_element_type=jnp.float32)
        .astype(jnp.bfloat16)
        .astype(jnp.float32)
        .reshape(nexp, slots, width)
    ).astype(jnp.bfloat16)
    weight_in, weight_out = (w_in[0], w_out[0])
    first_in, second_in, first_out, second_out = (m_in[0], v_in[0], m_out[0], v_out[0])
    other = migrate(
        (
            weight_in.astype(jnp.bfloat16),
            weight_out.astype(jnp.bfloat16),
            first_in,
            second_in,
            first_out,
            second_out,
        )
    )
    send_x, send_g, other = lax.optimization_barrier((send_x, send_g, other))
    other_w = (other[0].astype(weight_in.dtype), other[1].astype(weight_out.dtype))
    other_m = other[2:]
    weight_in = jnp.where(moved, other_w[0], weight_in)
    weight_out = jnp.where(moved, other_w[1], weight_out)
    first_in = jnp.where(moved, other_m[0], first_in)
    second_in = jnp.where(moved, other_m[1], second_in)
    first_out = jnp.where(moved, other_m[2], first_out)
    second_out = jnp.where(moved, other_m[3], second_out)
    recv_x, recv_g = (
        lax.all_to_all(send_x, "expert", split_axis=0, concat_axis=0, tiled=True),
        lax.all_to_all(send_g, "expert", split_axis=0, concat_axis=0, tiled=True),
    )
    rows = recv_x.reshape(-1, width)
    grows = recv_g.reshape(-1, width)
    wb_in = weight_in.astype(jnp.bfloat16)
    wb_out = weight_out.astype(jnp.bfloat16)
    pre = jnp.dot(rows, wb_in, preferred_element_type=jnp.float32)
    hidden, pull = jax.vjp(gelu_tanh, pre)
    hidden = hidden.astype(jnp.bfloat16)
    part = jnp.dot(hidden, wb_out, preferred_element_type=jnp.float32).astype(jnp.bfloat16)
    dhid = lax.dot_general(
        grows, wb_out, (((1,), (1,)), ((), ())), preferred_element_type=jnp.float32
    )
    dpre = pull(dhid)[0].astype(jnp.bfloat16)
    xpart = lax.dot_general(
        dpre, wb_in, (((1,), (1,)), ((), ())), preferred_element_type=jnp.float32
    ).astype(jnp.bfloat16)
    grad_in = lax.dot_general(
        rows, dpre, (((0,), (0,)), ((), ())), preferred_element_type=jnp.float32
    )
    grad_out = lax.dot_general(
        hidden, grows, (((0,), (0,)), ((), ())), preferred_element_type=jnp.float32
    )
    back_part, back_dx = (
        lax.all_to_all(
            part.reshape(nexp, slots, width), "expert", split_axis=0, concat_axis=0, tiled=True
        ),
        lax.all_to_all(
            xpart.reshape(nexp, slots, width), "expert", split_axis=0, concat_axis=0, tiled=True
        ),
    )
    grad_in, grad_out = lax.psum((grad_in, grad_out), "dp")
    new_w_in, new_m_in, new_v_in = adamw(weight_in, first_in, second_in, grad_in)
    new_w_out, new_m_out, new_v_out = adamw(weight_out, first_out, second_out, grad_out)
    row_expert = jnp.repeat(target_expert, slots)
    row_pos = jnp.tile(jnp.arange(slots, dtype=jnp.int32), nexp)
    owns = (
        kept[:, None]
        & (flat_routes[:, None] == row_expert[None, :])
        & (position[:, None] == row_pos[None, :])
    )
    owns_pair = owns.astype(jnp.bfloat16)
    owns_tok = owns.reshape(count, topk, nexp * slots).any(axis=1).astype(jnp.bfloat16)
    out_vals = jnp.dot(
        owns_pair, back_part.reshape(-1, width), preferred_element_type=jnp.float32
    )
    mixed = jnp.sum(out_vals.reshape(count, topk, width) * gates[:, :, None], axis=1).astype(
        jnp.bfloat16
    )
    token_grad = jnp.dot(
        owns_tok, back_dx.reshape(-1, width), preferred_element_type=jnp.float32
    ).astype(jnp.bfloat16)
    return (
        mixed,
        token_grad,
        new_w_in[None],
        new_w_out[None],
        new_m_in[None],
        new_v_in[None],
        new_m_out[None],
        new_v_out[None],
    )


def solution(mesh):
    in_specs = (
        P(("dp", "expert"), None),
        P(("dp", "expert"), None),
        P(("dp", "expert"), None),
        P(("dp", "expert"), None),
        P(),
        P(),
        P(),
        P("expert", None, None),
        P("expert", None, None),
        P("expert", None, None),
        P("expert", None, None),
        P("expert", None, None),
        P("expert", None, None),
    )
    out_specs = (
        P(("dp", "expert"), None),
        P(("dp", "expert"), None),
        P("expert", None, None),
        P("expert", None, None),
        P("expert", None, None),
        P("expert", None, None),
        P("expert", None, None),
        P("expert", None, None),
    )
    return jax.shard_map(local, mesh=mesh, in_specs=in_specs, out_specs=out_specs, check_vma=False)
```

```python
import jax
import jax.numpy as jnp
from jax import lax
from jax.sharding import PartitionSpec as P

GROUP = 4


def relay(block, step):
    ndp = lax.axis_size("dp")
    nexp = lax.axis_size("expert")
    route = []
    for d in range(ndp):
        sign = 1 if d % 2 == 0 else -1
        for e in range(nexp):
            route.append((d * nexp + e, d * nexp + (e + sign * step) % nexp))
    return lax.ppermute(block, ("dp", "expert"), route)


def migrate(groups):
    ndp = lax.axis_size("dp")
    step = lax.axis_size("expert") // 4
    here = lax.axis_index("dp")
    halves = tuple(
        lax.dynamic_slice_in_dim(g, here * (g.shape[1] // ndp), g.shape[1] // ndp, 1)
        for g in groups
    )
    moved = relay(halves, step)
    moved = relay(moved, step)
    return tuple(lax.all_gather(m, "dp", axis=1, tiled=True) for m in moved)


def gelu_tanh(value):
    return jax.nn.gelu(value, approximate=True)


def adamw(weight, first, second, grad):
    first_f = 0.9 * first.astype(jnp.float32) + 0.1 * grad
    second_f = 0.999 * second.astype(jnp.float32) + 0.001 * grad * grad
    corrected = first_f / (1.0 - 0.9**10) / (jnp.sqrt(second_f / (1.0 - 0.999**10)) + 1e-08)
    updated = weight - 0.01 * (corrected + 0.1 * weight)
    return (updated, first_f.astype(jnp.bfloat16), second_f.astype(jnp.bfloat16))


def body(
    tokens,
    cotangent,
    routes,
    gates,
    capacity,
    layout,
    partner,
    w_in,
    w_out,
    m_in,
    v_in,
    m_out,
    v_out,
):
    width = tokens.shape[1]
    count = tokens.shape[0]
    topk = routes.shape[1]
    experts = capacity.shape[0]
    slots = 3 * count * topk // (2 * experts)
    nexp = lax.axis_size("expert")
    here = lax.axis_index("expert")
    moved = jnp.take(partner, here) != here
    flat_routes = routes.reshape(-1)
    onehot = (flat_routes[:, None] == jnp.arange(experts, dtype=jnp.int32)[None, :]).astype(
        jnp.int32
    )
    position = jnp.sum((jnp.cumsum(onehot, 0) - 1) * onehot, 1)
    limit = jnp.sum(onehot * capacity[None, :], 1)
    kept = position < limit
    npairs = count * topk
    slot = jnp.where(kept, flat_routes * slots + position, experts * slots)
    pair_of = (
        jnp.full((experts * slots + 1,), npairs, jnp.int32)
        .at[slot]
        .set(jnp.arange(npairs, dtype=jnp.int32))[:-1]
        .reshape(experts, slots)
    )
    held = jnp.take(layout, partner, axis=0)
    target_expert = held // GROUP
    send_pair = jnp.take(pair_of, target_expert, axis=0)
    send_tok = jnp.where(send_pair < npairs, send_pair // topk, count)
    gate_of = jnp.concatenate([gates.reshape(-1), jnp.zeros((1,), gates.dtype)])
    pick = (send_tok[:, :, None] == jnp.arange(count, dtype=jnp.int32)[None, None, :]).astype(
        jnp.bfloat16
    )
    pick = pick.reshape(nexp * slots, count)
    send_x = (
        jnp.dot(pick, tokens, preferred_element_type=jnp.float32)
        .astype(jnp.bfloat16)
        .reshape(nexp, slots, width)
    )
    send_g = (
        jnp.take(gate_of, send_pair)[:, :, None]
        * jnp.dot(pick, cotangent, preferred_element_type=jnp.float32)
        .astype(jnp.bfloat16)
        .astype(jnp.float32)
        .reshape(nexp, slots, width)
    ).astype(jnp.bfloat16)
    weight_in, weight_out = (w_in[0], w_out[0])
    first_in, second_in, first_out, second_out = (m_in[0], v_in[0], m_out[0], v_out[0])
    group_in, group_out = migrate(
        (
            jnp.stack([weight_in.astype(jnp.bfloat16), first_in, second_in]),
            jnp.stack([weight_out.astype(jnp.bfloat16), first_out, second_out]),
        )
    )
    other = (group_in[0], group_out[0], group_in[1], group_in[2], group_out[1], group_out[2])
    send_x, send_g, other = lax.optimization_barrier((send_x, send_g, other))
    other_w = (other[0].astype(weight_in.dtype), other[1].astype(weight_out.dtype))
    other_m = other[2:]
    weight_in = jnp.where(moved, other_w[0], weight_in)
    weight_out = jnp.where(moved, other_w[1], weight_out)
    first_in = jnp.where(moved, other_m[0], first_in)
    second_in = jnp.where(moved, other_m[1], second_in)
    first_out = jnp.where(moved, other_m[2], first_out)
    second_out = jnp.where(moved, other_m[3], second_out)
    recv_x, recv_g = (
        lax.all_to_all(send_x, "expert", split_axis=0, concat_axis=0, tiled=True),
        lax.all_to_all(send_g, "expert", split_axis=0, concat_axis=0, tiled=True),
    )
    rows = recv_x.reshape(-1, width)
    grows = recv_g.reshape(-1, width)
    wb_in = weight_in.astype(jnp.bfloat16)
    wb_out = weight_out.astype(jnp.bfloat16)
    pre = jnp.dot(rows, wb_in, preferred_element_type=jnp.float32)
    hidden, pull = jax.vjp(gelu_tanh, pre)
    hidden = hidden.astype(jnp.bfloat16)
    part = jnp.dot(hidden, wb_out, preferred_element_type=jnp.float32).astype(jnp.bfloat16)
    dhid = lax.dot_general(
        grows, wb_out, (((1,), (1,)), ((), ())), preferred_element_type=jnp.float32
    )
    dpre = pull(dhid)[0].astype(jnp.bfloat16)
    xpart = lax.dot_general(
        dpre, wb_in, (((1,), (1,)), ((), ())), preferred_element_type=jnp.float32
    ).astype(jnp.bfloat16)
    grad_in = lax.dot_general(
        rows, dpre, (((0,), (0,)), ((), ())), preferred_element_type=jnp.float32
    )
    grad_out = lax.dot_general(
        hidden, grows, (((0,), (0,)), ((), ())), preferred_element_type=jnp.float32
    )
    back_part, back_dx = (
        lax.all_to_all(
            part.reshape(nexp, slots, width), "expert", split_axis=0, concat_axis=0, tiled=True
        ),
        lax.all_to_all(
            xpart.reshape(nexp, slots, width), "expert", split_axis=0, concat_axis=0, tiled=True
        ),
    )
    grad_in, grad_out = lax.psum((grad_in, grad_out), "dp")
    new_w_in, new_m_in, new_v_in = adamw(weight_in, first_in, second_in, grad_in)
    new_w_out, new_m_out, new_v_out = adamw(weight_out, first_out, second_out, grad_out)
    row_expert = jnp.repeat(target_expert, slots)
    row_pos = jnp.tile(jnp.arange(slots, dtype=jnp.int32), nexp)
    owns = (
        kept[:, None]
        & (flat_routes[:, None] == row_expert[None, :])
        & (position[:, None] == row_pos[None, :])
    )
    owns_pair = owns.astype(jnp.bfloat16)
    owns_tok = owns.reshape(count, topk, nexp * slots).any(axis=1).astype(jnp.bfloat16)
    out_vals = jnp.dot(
        owns_pair, back_part.reshape(-1, width), preferred_element_type=jnp.float32
    )
    mixed = jnp.sum(out_vals.reshape(count, topk, width) * gates[:, :, None], axis=1).astype(
        jnp.bfloat16
    )
    token_grad = jnp.dot(
        owns_tok, back_dx.reshape(-1, width), preferred_element_type=jnp.float32
    ).astype(jnp.bfloat16)
    return (
        mixed,
        token_grad,
        new_w_in[None],
        new_w_out[None],
        new_m_in[None],
        new_v_in[None],
        new_m_out[None],
        new_v_out[None],
    )


def solution(mesh):
    in_specs = (
        P(("dp", "expert"), None),
        P(("dp", "expert"), None),
        P(("dp", "expert"), None),
        P(("dp", "expert"), None),
        P(),
        P(),
        P(),
        P("expert", None, None),
        P("expert", None, None),
        P("expert", None, None),
        P("expert", None, None),
        P("expert", None, None),
        P("expert", None, None),
    )
    out_specs = (
        P(("dp", "expert"), None),
        P(("dp", "expert"), None),
        P("expert", None, None),
        P("expert", None, None),
        P("expert", None, None),
        P("expert", None, None),
        P("expert", None, None),
        P("expert", None, None),
    )
    return jax.shard_map(body, mesh=mesh, in_specs=in_specs, out_specs=out_specs, check_vma=False)
```

```python
import jax
import jax.numpy as jnp
from jax import lax
from jax.sharding import PartitionSpec as P

GROUP = 4


def relay(block, step):
    ndp = lax.axis_size("dp")
    nexp = lax.axis_size("expert")
    route = []
    for d in range(ndp):
        sign = 1 if d % 2 == 0 else -1
        for e in range(nexp):
            route.append((d * nexp + e, d * nexp + (e + sign * step) % nexp))
    return lax.ppermute(block, ("dp", "expert"), route)


def migrate(groups):
    ndp = lax.axis_size("dp")
    step = lax.axis_size("expert") // 4
    here = lax.axis_index("dp")
    halves = tuple(
        lax.dynamic_slice_in_dim(g, here * (g.shape[1] // ndp), g.shape[1] // ndp, 1)
        for g in groups
    )
    moved = relay(halves, step)
    moved = relay(moved, step)
    return moved


def join(moved):
    return tuple(lax.all_gather(m, "dp", axis=1, tiled=True) for m in moved)


def gelu_tanh(value):
    return jax.nn.gelu(value, approximate=True)


def adamw(weight, first, second, grad):
    first_f = 0.9 * first.astype(jnp.float32) + 0.1 * grad
    second_f = 0.999 * second.astype(jnp.float32) + 0.001 * grad * grad
    corrected = first_f / (1.0 - 0.9**10) / (jnp.sqrt(second_f / (1.0 - 0.999**10)) + 1e-08)
    updated = weight - 0.01 * (corrected + 0.1 * weight)
    return (updated, first_f.astype(jnp.bfloat16), second_f.astype(jnp.bfloat16))


def body(
    tokens,
    cotangent,
    routes,
    gates,
    capacity,
    layout,
    partner,
    w_in,
    w_out,
    m_in,
    v_in,
    m_out,
    v_out,
):
    width = tokens.shape[1]
    count = tokens.shape[0]
    topk = routes.shape[1]
    experts = capacity.shape[0]
    slots = 3 * count * topk // (2 * experts)
    nexp = lax.axis_size("expert")
    here = lax.axis_index("expert")
    moved = jnp.take(partner, here) != here
    flat_routes = routes.reshape(-1)
    onehot = (flat_routes[:, None] == jnp.arange(experts, dtype=jnp.int32)[None, :]).astype(
        jnp.int32
    )
    position = jnp.sum((jnp.cumsum(onehot, 0) - 1) * onehot, 1)
    limit = jnp.sum(onehot * capacity[None, :], 1)
    kept = position < limit
    npairs = count * topk
    slot = jnp.where(kept, flat_routes * slots + position, experts * slots)
    pair_of = (
        jnp.full((experts * slots + 1,), npairs, jnp.int32)
        .at[slot]
        .set(jnp.arange(npairs, dtype=jnp.int32))[:-1]
        .reshape(experts, slots)
    )
    held = jnp.take(layout, partner, axis=0)
    target_expert = held // GROUP
    send_pair = jnp.take(pair_of, target_expert, axis=0)
    send_tok = jnp.where(send_pair < npairs, send_pair // topk, count)
    gate_of = jnp.concatenate([gates.reshape(-1), jnp.zeros((1,), gates.dtype)])
    pick = (send_tok[:, :, None] == jnp.arange(count, dtype=jnp.int32)[None, None, :]).astype(
        jnp.bfloat16
    )
    pick = pick.reshape(nexp * slots, count)
    send_x = (
        jnp.dot(pick, tokens, preferred_element_type=jnp.float32)
        .astype(jnp.bfloat16)
        .reshape(nexp, slots, width)
    )
    send_g = (
        jnp.take(gate_of, send_pair)[:, :, None]
        * jnp.dot(pick, cotangent, preferred_element_type=jnp.float32)
        .astype(jnp.bfloat16)
        .astype(jnp.float32)
        .reshape(nexp, slots, width)
    ).astype(jnp.bfloat16)
    weight_in, weight_out = (w_in[0], w_out[0])
    first_in, second_in, first_out, second_out = (m_in[0], v_in[0], m_out[0], v_out[0])
    halves = migrate(
        (
            jnp.stack([weight_in.astype(jnp.bfloat16), first_in, second_in]),
            jnp.stack([weight_out.astype(jnp.bfloat16), first_out, second_out]),
        )
    )
    send_x, send_g, halves = lax.optimization_barrier((send_x, send_g, halves))
    group_in, group_out = join(halves)
    other = (group_in[0], group_out[0], group_in[1], group_in[2], group_out[1], group_out[2])
    other_w = (other[0].astype(weight_in.dtype), other[1].astype(weight_out.dtype))
    other_m = other[2:]
    weight_in = jnp.where(moved, other_w[0], weight_in)
    weight_out = jnp.where(moved, other_w[1], weight_out)
    first_in = jnp.where(moved, other_m[0], first_in)
    second_in = jnp.where(moved, other_m[1], second_in)
    first_out = jnp.where(moved, other_m[2], first_out)
    second_out = jnp.where(moved, other_m[3], second_out)
    recv_x, recv_g = (
        lax.all_to_all(send_x, "expert", split_axis=0, concat_axis=0, tiled=True),
        lax.all_to_all(send_g, "expert", split_axis=0, concat_axis=0, tiled=True),
    )
    rows = recv_x.reshape(-1, width)
    grows = recv_g.reshape(-1, width)
    wb_in = weight_in.astype(jnp.bfloat16)
    wb_out = weight_out.astype(jnp.bfloat16)
    pre = jnp.dot(rows, wb_in, preferred_element_type=jnp.float32)
    hidden, pull = jax.vjp(gelu_tanh, pre)
    hidden = hidden.astype(jnp.bfloat16)
    part = jnp.dot(hidden, wb_out, preferred_element_type=jnp.float32).astype(jnp.bfloat16)
    dhid = lax.dot_general(
        grows, wb_out, (((1,), (1,)), ((), ())), preferred_element_type=jnp.float32
    )
    dpre = pull(dhid)[0].astype(jnp.bfloat16)
    xpart = lax.dot_general(
        dpre, wb_in, (((1,), (1,)), ((), ())), preferred_element_type=jnp.float32
    ).astype(jnp.bfloat16)
    grad_in = lax.dot_general(
        rows, dpre, (((0,), (0,)), ((), ())), preferred_element_type=jnp.float32
    )
    grad_out = lax.dot_general(
        hidden, grows, (((0,), (0,)), ((), ())), preferred_element_type=jnp.float32
    )
    back_part, back_dx = (
        lax.all_to_all(
            part.reshape(nexp, slots, width), "expert", split_axis=0, concat_axis=0, tiled=True
        ),
        lax.all_to_all(
            xpart.reshape(nexp, slots, width), "expert", split_axis=0, concat_axis=0, tiled=True
        ),
    )
    grad_in, grad_out = lax.psum((grad_in, grad_out), "dp")
    new_w_in, new_m_in, new_v_in = adamw(weight_in, first_in, second_in, grad_in)
    new_w_out, new_m_out, new_v_out = adamw(weight_out, first_out, second_out, grad_out)
    row_expert = jnp.repeat(target_expert, slots)
    row_pos = jnp.tile(jnp.arange(slots, dtype=jnp.int32), nexp)
    owns = (
        kept[:, None]
        & (flat_routes[:, None] == row_expert[None, :])
        & (position[:, None] == row_pos[None, :])
    )
    owns_pair = owns.astype(jnp.bfloat16)
    owns_tok = owns.reshape(count, topk, nexp * slots).any(axis=1).astype(jnp.bfloat16)
    out_vals = jnp.dot(
        owns_pair, back_part.reshape(-1, width), preferred_element_type=jnp.float32
    )
    mixed = jnp.sum(out_vals.reshape(count, topk, width) * gates[:, :, None], axis=1).astype(
        jnp.bfloat16
    )
    token_grad = jnp.dot(
        owns_tok, back_dx.reshape(-1, width), preferred_element_type=jnp.float32
    ).astype(jnp.bfloat16)
    return (
        mixed,
        token_grad,
        new_w_in[None],
        new_w_out[None],
        new_m_in[None],
        new_v_in[None],
        new_m_out[None],
        new_v_out[None],
    )


def solution(mesh):
    in_specs = (
        P(("dp", "expert"), None),
        P(("dp", "expert"), None),
        P(("dp", "expert"), None),
        P(("dp", "expert"), None),
        P(),
        P(),
        P(),
        P("expert", None, None),
        P("expert", None, None),
        P("expert", None, None),
        P("expert", None, None),
        P("expert", None, None),
        P("expert", None, None),
    )
    out_specs = (
        P(("dp", "expert"), None),
        P(("dp", "expert"), None),
        P("expert", None, None),
        P("expert", None, None),
        P("expert", None, None),
        P("expert", None, None),
        P("expert", None, None),
        P("expert", None, None),
    )
    return jax.shard_map(body, mesh=mesh, in_specs=in_specs, out_specs=out_specs, check_vma=False)
```

```python
import jax
import jax.numpy as jnp
from jax import lax
from jax.sharding import PartitionSpec as P

GROUP = 4


def relay(block, step):
    ndp = lax.axis_size("dp")
    nexp = lax.axis_size("expert")
    route = []
    for d in range(ndp):
        sign = 1 if d % 2 == 0 else -1
        for e in range(nexp):
            route.append((d * nexp + e, d * nexp + (e + sign * step) % nexp))
    return lax.ppermute(block, ("dp", "expert"), route)


def migrate(groups):
    ndp = lax.axis_size("dp")
    step = lax.axis_size("expert") // 4
    here = lax.axis_index("dp")
    halves = tuple(
        lax.dynamic_slice_in_dim(g, here * (g.shape[1] // ndp), g.shape[1] // ndp, 1)
        for g in groups
    )
    moved = relay(halves, step)
    moved = relay(moved, step)
    return moved


def join(moved):
    return tuple(lax.all_gather(m, "dp", axis=1, tiled=True) for m in moved)


def gelu_tanh(value):
    return jax.nn.gelu(value, approximate=True)


def adamw(weight, first, second, grad):
    first_f = 0.9 * first.astype(jnp.float32) + 0.1 * grad
    second_f = 0.999 * second.astype(jnp.float32) + 0.001 * grad * grad
    corrected = first_f / (1.0 - 0.9**10) / (jnp.sqrt(second_f / (1.0 - 0.999**10)) + 1e-08)
    updated = weight - 0.01 * (corrected + 0.1 * weight)
    return (updated, first_f.astype(jnp.bfloat16), second_f.astype(jnp.bfloat16))


def body(
    tokens,
    cotangent,
    routes,
    gates,
    capacity,
    layout,
    partner,
    w_in,
    w_out,
    m_in,
    v_in,
    m_out,
    v_out,
):
    width = tokens.shape[1]
    count = tokens.shape[0]
    topk = routes.shape[1]
    experts = capacity.shape[0]
    slots = 3 * count * topk // (2 * experts)
    nexp = lax.axis_size("expert")
    here = lax.axis_index("expert")
    moved = jnp.take(partner, here) != here
    flat_routes = routes.reshape(-1)
    onehot = (flat_routes[:, None] == jnp.arange(experts, dtype=jnp.int32)[None, :]).astype(
        jnp.int32
    )
    position = jnp.sum((jnp.cumsum(onehot, 0) - 1) * onehot, 1)
    limit = jnp.sum(onehot * capacity[None, :], 1)
    kept = position < limit
    npairs = count * topk
    slot = jnp.where(kept, flat_routes * slots + position, experts * slots)
    pair_of = (
        jnp.full((experts * slots + 1,), npairs, jnp.int32)
        .at[slot]
        .set(jnp.arange(npairs, dtype=jnp.int32))[:-1]
        .reshape(experts, slots)
    )
    held = jnp.take(layout, partner, axis=0)
    target_expert = held // GROUP
    send_pair = jnp.take(pair_of, target_expert, axis=0)
    send_tok = jnp.where(send_pair < npairs, send_pair // topk, count)
    gate_of = jnp.concatenate([gates.reshape(-1), jnp.zeros((1,), gates.dtype)])
    pick = (send_tok[:, :, None] == jnp.arange(count, dtype=jnp.int32)[None, None, :]).astype(
        jnp.bfloat16
    )
    pick = pick.reshape(nexp * slots, count)
    send_x = (
        jnp.dot(pick, tokens, preferred_element_type=jnp.float32)
        .astype(jnp.bfloat16)
        .reshape(nexp, slots, width)
    )
    send_g = (
        jnp.take(gate_of, send_pair)[:, :, None]
        * jnp.dot(pick, cotangent, preferred_element_type=jnp.float32)
        .astype(jnp.bfloat16)
        .astype(jnp.float32)
        .reshape(nexp, slots, width)
    ).astype(jnp.bfloat16)
    weight_in, weight_out = (w_in[0], w_out[0])
    first_in, second_in, first_out, second_out = (m_in[0], v_in[0], m_out[0], v_out[0])
    halves = migrate(
        (
            jnp.stack([weight_in.astype(jnp.bfloat16), first_in, second_in]),
            jnp.stack([weight_out.astype(jnp.bfloat16), first_out, second_out]),
        )
    )
    send_x, send_g, halves = lax.optimization_barrier((send_x, send_g, halves))
    group_in, group_out = join(halves)
    other = (group_in[0], group_out[0], group_in[1], group_in[2], group_out[1], group_out[2])
    other_w = (other[0].astype(weight_in.dtype), other[1].astype(weight_out.dtype))
    other_m = other[2:]
    weight_in = jnp.where(moved, other_w[0], weight_in)
    weight_out = jnp.where(moved, other_w[1], weight_out)
    first_in = jnp.where(moved, other_m[0], first_in)
    second_in = jnp.where(moved, other_m[1], second_in)
    first_out = jnp.where(moved, other_m[2], first_out)
    second_out = jnp.where(moved, other_m[3], second_out)
    recv = lax.all_to_all(
        jnp.stack([send_x, send_g], axis=1), "expert", split_axis=0, concat_axis=0, tiled=True
    )
    rows = recv[:, 0].reshape(-1, width)
    grows = recv[:, 1].reshape(-1, width)
    wb_in = weight_in.astype(jnp.bfloat16)
    wb_out = weight_out.astype(jnp.bfloat16)
    pre = jnp.dot(rows, wb_in, preferred_element_type=jnp.float32)
    hidden, pull = jax.vjp(gelu_tanh, pre)
    hidden = hidden.astype(jnp.bfloat16)
    part = jnp.dot(hidden, wb_out, preferred_element_type=jnp.float32).astype(jnp.bfloat16)
    dhid = lax.dot_general(
        grows, wb_out, (((1,), (1,)), ((), ())), preferred_element_type=jnp.float32
    )
    dpre = pull(dhid)[0].astype(jnp.bfloat16)
    xpart = lax.dot_general(
        dpre, wb_in, (((1,), (1,)), ((), ())), preferred_element_type=jnp.float32
    ).astype(jnp.bfloat16)
    grad_in = lax.dot_general(
        rows, dpre, (((0,), (0,)), ((), ())), preferred_element_type=jnp.float32
    )
    grad_out = lax.dot_general(
        hidden, grows, (((0,), (0,)), ((), ())), preferred_element_type=jnp.float32
    )
    back = lax.all_to_all(
        jnp.stack(
            [part.reshape(nexp, slots, width), xpart.reshape(nexp, slots, width)], axis=1
        ),
        "expert",
        split_axis=0,
        concat_axis=0,
        tiled=True,
    )
    back_part = back[:, 0]
    back_dx = back[:, 1]
    grad_in, grad_out = lax.psum((grad_in, grad_out), "dp")
    new_w_in, new_m_in, new_v_in = adamw(weight_in, first_in, second_in, grad_in)
    new_w_out, new_m_out, new_v_out = adamw(weight_out, first_out, second_out, grad_out)
    row_expert = jnp.repeat(target_expert, slots)
    row_pos = jnp.tile(jnp.arange(slots, dtype=jnp.int32), nexp)
    owns = (
        kept[:, None]
        & (flat_routes[:, None] == row_expert[None, :])
        & (position[:, None] == row_pos[None, :])
    )
    owns_pair = owns.astype(jnp.bfloat16)
    owns_tok = owns.reshape(count, topk, nexp * slots).any(axis=1).astype(jnp.bfloat16)
    out_vals = jnp.dot(
        owns_pair, back_part.reshape(-1, width), preferred_element_type=jnp.float32
    )
    mixed = jnp.sum(out_vals.reshape(count, topk, width) * gates[:, :, None], axis=1).astype(
        jnp.bfloat16
    )
    token_grad = jnp.dot(
        owns_tok, back_dx.reshape(-1, width), preferred_element_type=jnp.float32
    ).astype(jnp.bfloat16)
    return (
        mixed,
        token_grad,
        new_w_in[None],
        new_w_out[None],
        new_m_in[None],
        new_v_in[None],
        new_m_out[None],
        new_v_out[None],
    )


def solution(mesh):
    in_specs = (
        P(("dp", "expert"), None),
        P(("dp", "expert"), None),
        P(("dp", "expert"), None),
        P(("dp", "expert"), None),
        P(),
        P(),
        P(),
        P("expert", None, None),
        P("expert", None, None),
        P("expert", None, None),
        P("expert", None, None),
        P("expert", None, None),
        P("expert", None, None),
    )
    out_specs = (
        P(("dp", "expert"), None),
        P(("dp", "expert"), None),
        P("expert", None, None),
        P("expert", None, None),
        P("expert", None, None),
        P("expert", None, None),
        P("expert", None, None),
        P("expert", None, None),
    )
    return jax.shard_map(body, mesh=mesh, in_specs=in_specs, out_specs=out_specs, check_vma=False)
```

```python
import jax
import jax.numpy as jnp
from jax import lax
from jax.sharding import PartitionSpec as P

GROUP = 4


def relay(block, step, both=True):
    ndp = lax.axis_size("dp")
    nexp = lax.axis_size("expert")
    route = []
    for d in range(ndp):
        sign = 1 if d % 2 == 0 and both else -1
        for e in range(nexp):
            route.append((d * nexp + e, d * nexp + (e + sign * step) % nexp))
    return lax.ppermute(block, ("dp", "expert"), route)


def migrate(groups, both=True):
    ndp = lax.axis_size("dp")
    step = lax.axis_size("expert") // 4
    here = lax.axis_index("dp")
    halves = tuple(
        lax.dynamic_slice_in_dim(g, here * (g.shape[1] // ndp), g.shape[1] // ndp, 1)
        for g in groups
    )
    moved = relay(halves, step, both)
    moved = relay(moved, step, both)
    return moved


def join(moved):
    return tuple(lax.all_gather(m, "dp", axis=1, tiled=True) for m in moved)


def gelu_tanh(value):
    return jax.nn.gelu(value, approximate=True)


def adamw(weight, first, second, grad):
    first_f = 0.9 * first.astype(jnp.float32) + 0.1 * grad
    second_f = 0.999 * second.astype(jnp.float32) + 0.001 * grad * grad
    corrected = first_f / (1.0 - 0.9**10) / (jnp.sqrt(second_f / (1.0 - 0.999**10)) + 1e-08)
    updated = weight - 0.01 * (corrected + 0.1 * weight)
    return (updated, first_f.astype(jnp.bfloat16), second_f.astype(jnp.bfloat16))


def body(
    tokens,
    cotangent,
    routes,
    gates,
    capacity,
    layout,
    partner,
    w_in,
    w_out,
    m_in,
    v_in,
    m_out,
    v_out,
):
    width = tokens.shape[1]
    count = tokens.shape[0]
    topk = routes.shape[1]
    experts = capacity.shape[0]
    slots = 3 * count * topk // (2 * experts)
    nexp = lax.axis_size("expert")
    here = lax.axis_index("expert")
    moved = jnp.take(partner, here) != here
    flat_routes = routes.reshape(-1)
    onehot = (flat_routes[:, None] == jnp.arange(experts, dtype=jnp.int32)[None, :]).astype(
        jnp.int32
    )
    position = jnp.sum((jnp.cumsum(onehot, 0) - 1) * onehot, 1)
    limit = jnp.sum(onehot * capacity[None, :], 1)
    kept = position < limit
    npairs = count * topk
    slot = jnp.where(kept, flat_routes * slots + position, experts * slots)
    pair_of = (
        jnp.full((experts * slots + 1,), npairs, jnp.int32)
        .at[slot]
        .set(jnp.arange(npairs, dtype=jnp.int32))[:-1]
        .reshape(experts, slots)
    )
    held = jnp.take(layout, partner, axis=0)
    target_expert = held // GROUP
    send_pair = jnp.take(pair_of, target_expert, axis=0)
    send_tok = jnp.where(send_pair < npairs, send_pair // topk, count)
    gate_of = jnp.concatenate([gates.reshape(-1), jnp.zeros((1,), gates.dtype)])
    pick = (send_tok[:, :, None] == jnp.arange(count, dtype=jnp.int32)[None, None, :]).astype(
        jnp.bfloat16
    )
    pick = pick.reshape(nexp * slots, count)
    send_x = (
        jnp.dot(pick, tokens, preferred_element_type=jnp.float32)
        .astype(jnp.bfloat16)
        .reshape(nexp, slots, width)
    )
    send_g = (
        jnp.take(gate_of, send_pair)[:, :, None]
        * jnp.dot(pick, cotangent, preferred_element_type=jnp.float32)
        .astype(jnp.bfloat16)
        .astype(jnp.float32)
        .reshape(nexp, slots, width)
    ).astype(jnp.bfloat16)
    weight_in, weight_out = (w_in[0], w_out[0])
    first_in, second_in, first_out, second_out = (m_in[0], v_in[0], m_out[0], v_out[0])
    halves = migrate(
        (weight_in.astype(jnp.bfloat16)[None], weight_out.astype(jnp.bfloat16)[None])
    )
    send_x, send_g, halves = lax.optimization_barrier((send_x, send_g, halves))
    group_in, group_out = join(halves)
    recv_x = lax.all_to_all(send_x, "expert", split_axis=0, concat_axis=0, tiled=True)
    recv_x, moments = lax.optimization_barrier(
        (recv_x, (jnp.stack([first_in, second_in]), jnp.stack([first_out, second_out])))
    )
    moment_in, moment_out = join(migrate(moments, False))
    other = (group_in[0], group_out[0], moment_in[0], moment_in[1], moment_out[0], moment_out[1])
    other_w = (other[0].astype(weight_in.dtype), other[1].astype(weight_out.dtype))
    other_m = other[2:]
    weight_in = jnp.where(moved, other_w[0], weight_in)
    weight_out = jnp.where(moved, other_w[1], weight_out)
    first_in = jnp.where(moved, other_m[0], first_in)
    second_in = jnp.where(moved, other_m[1], second_in)
    first_out = jnp.where(moved, other_m[2], first_out)
    second_out = jnp.where(moved, other_m[3], second_out)
    recv_g = lax.all_to_all(send_g, "expert", split_axis=0, concat_axis=0, tiled=True)
    rows = recv_x.reshape(-1, width)
    grows = recv_g.reshape(-1, width)
    wb_in = weight_in.astype(jnp.bfloat16)
    wb_out = weight_out.astype(jnp.bfloat16)
    pre = jnp.dot(rows, wb_in, preferred_element_type=jnp.float32)
    hidden, pull = jax.vjp(gelu_tanh, pre)
    hidden = hidden.astype(jnp.bfloat16)
    part = jnp.dot(hidden, wb_out, preferred_element_type=jnp.float32).astype(jnp.bfloat16)
    dhid = lax.dot_general(
        grows, wb_out, (((1,), (1,)), ((), ())), preferred_element_type=jnp.float32
    )
    dpre = pull(dhid)[0].astype(jnp.bfloat16)
    xpart = lax.dot_general(
        dpre, wb_in, (((1,), (1,)), ((), ())), preferred_element_type=jnp.float32
    ).astype(jnp.bfloat16)
    grad_in = lax.dot_general(
        rows, dpre, (((0,), (0,)), ((), ())), preferred_element_type=jnp.float32
    )
    grad_out = lax.dot_general(
        hidden, grows, (((0,), (0,)), ((), ())), preferred_element_type=jnp.float32
    )
    back_part, back_dx = (
        lax.all_to_all(
            part.reshape(nexp, slots, width), "expert", split_axis=0, concat_axis=0, tiled=True
        ),
        lax.all_to_all(
            xpart.reshape(nexp, slots, width), "expert", split_axis=0, concat_axis=0, tiled=True
        ),
    )
    grad_in, grad_out = lax.psum((grad_in, grad_out), "dp")
    new_w_in, new_m_in, new_v_in = adamw(weight_in, first_in, second_in, grad_in)
    new_w_out, new_m_out, new_v_out = adamw(weight_out, first_out, second_out, grad_out)
    row_expert = jnp.repeat(target_expert, slots)
    row_pos = jnp.tile(jnp.arange(slots, dtype=jnp.int32), nexp)
    owns = (
        kept[:, None]
        & (flat_routes[:, None] == row_expert[None, :])
        & (position[:, None] == row_pos[None, :])
    )
    owns_pair = owns.astype(jnp.bfloat16)
    owns_tok = owns.reshape(count, topk, nexp * slots).any(axis=1).astype(jnp.bfloat16)
    out_vals = jnp.dot(
        owns_pair, back_part.reshape(-1, width), preferred_element_type=jnp.float32
    )
    mixed = jnp.sum(out_vals.reshape(count, topk, width) * gates[:, :, None], axis=1).astype(
        jnp.bfloat16
    )
    token_grad = jnp.dot(
        owns_tok, back_dx.reshape(-1, width), preferred_element_type=jnp.float32
    ).astype(jnp.bfloat16)
    return (
        mixed,
        token_grad,
        new_w_in[None],
        new_w_out[None],
        new_m_in[None],
        new_v_in[None],
        new_m_out[None],
        new_v_out[None],
    )


def solution(mesh):
    in_specs = (
        P(("dp", "expert"), None),
        P(("dp", "expert"), None),
        P(("dp", "expert"), None),
        P(("dp", "expert"), None),
        P(),
        P(),
        P(),
        P("expert", None, None),
        P("expert", None, None),
        P("expert", None, None),
        P("expert", None, None),
        P("expert", None, None),
        P("expert", None, None),
    )
    out_specs = (
        P(("dp", "expert"), None),
        P(("dp", "expert"), None),
        P("expert", None, None),
        P("expert", None, None),
        P("expert", None, None),
        P("expert", None, None),
        P("expert", None, None),
        P("expert", None, None),
    )
    return jax.shard_map(body, mesh=mesh, in_specs=in_specs, out_specs=out_specs, check_vma=False)
```

```python
import jax
import jax.numpy as jnp
from jax import lax
from jax.sharding import PartitionSpec as P

GROUP = 4


def relay(block, step):
    ndp = lax.axis_size("dp")
    nexp = lax.axis_size("expert")
    route = []
    for d in range(ndp):
        sign = 1 if d % 2 == 0 else -1
        for e in range(nexp):
            route.append((d * nexp + e, d * nexp + (e + sign * step) % nexp))
    return lax.ppermute(block, ("dp", "expert"), route)


def migrate(groups):
    ndp = lax.axis_size("dp")
    step = lax.axis_size("expert") // 4
    here = lax.axis_index("dp")
    halves = tuple(
        jnp.stack(
            [
                lax.dynamic_slice_in_dim(a, here * (a.shape[0] // ndp), a.shape[0] // ndp, 0)
                .astype(jnp.bfloat16)
                for a in g
            ]
        )
        for g in groups
    )
    moved = relay(halves, step)
    moved = relay(moved, step)
    return moved


def join(moved):
    return tuple(lax.all_gather(m, "dp", axis=1, tiled=True) for m in moved)


def gelu_tanh(value):
    return jax.nn.gelu(value, approximate=True)


def adamw(weight, first, second, grad):
    first_f = 0.9 * first.astype(jnp.float32) + 0.1 * grad
    second_f = 0.999 * second.astype(jnp.float32) + 0.001 * grad * grad
    corrected = first_f / (1.0 - 0.9**10) / (jnp.sqrt(second_f / (1.0 - 0.999**10)) + 1e-08)
    updated = weight - 0.01 * (corrected + 0.1 * weight)
    return (updated, first_f.astype(jnp.bfloat16), second_f.astype(jnp.bfloat16))


def body(
    tokens,
    cotangent,
    routes,
    gates,
    capacity,
    layout,
    partner,
    w_in,
    w_out,
    m_in,
    v_in,
    m_out,
    v_out,
):
    width = tokens.shape[1]
    count = tokens.shape[0]
    topk = routes.shape[1]
    experts = capacity.shape[0]
    slots = 3 * count * topk // (2 * experts)
    nexp = lax.axis_size("expert")
    here = lax.axis_index("expert")
    moved = jnp.take(partner, here) != here
    flat_routes = routes.reshape(-1)
    onehot = (flat_routes[:, None] == jnp.arange(experts, dtype=jnp.int32)[None, :]).astype(
        jnp.int32
    )
    position = jnp.sum((jnp.cumsum(onehot, 0) - 1) * onehot, 1)
    limit = jnp.sum(onehot * capacity[None, :], 1)
    kept = position < limit
    held = jnp.take(layout, partner, axis=0)
    target_expert = held // GROUP
    row_expert = jnp.repeat(target_expert, slots)
    row_pos = jnp.tile(jnp.arange(slots, dtype=jnp.int32), nexp)
    owns = (
        kept[:, None]
        & (flat_routes[:, None] == row_expert[None, :])
        & (position[:, None] == row_pos[None, :])
    )
    owns_tok = owns.reshape(count, topk, nexp * slots).any(axis=1).astype(jnp.bfloat16)
    gate_row = jnp.sum(jnp.where(owns, gates.reshape(-1)[:, None], 0.0), axis=0)
    pick_dims = (((0,), (0,)), ((), ()))
    send_x = (
        lax.dot_general(owns_tok, tokens, pick_dims, preferred_element_type=jnp.float32)
        .astype(jnp.bfloat16)
        .reshape(nexp, slots, width)
    )
    send_g = (
        gate_row.reshape(nexp, slots)[:, :, None]
        * lax.dot_general(owns_tok, cotangent, pick_dims, preferred_element_type=jnp.float32)
        .astype(jnp.bfloat16)
        .astype(jnp.float32)
        .reshape(nexp, slots, width)
    ).astype(jnp.bfloat16)
    weight_in, weight_out = (w_in[0], w_out[0])
    first_in, second_in, first_out, second_out = (m_in[0], v_in[0], m_out[0], v_out[0])
    halves = migrate(((weight_in, first_in, second_in), (weight_out, first_out, second_out)))
    send_x, send_g, halves = lax.optimization_barrier((send_x, send_g, halves))
    group_in, group_out = join(halves)
    other = (group_in[0], group_out[0], group_in[1], group_in[2], group_out[1], group_out[2])
    other_w = (other[0].astype(weight_in.dtype), other[1].astype(weight_out.dtype))
    other_m = other[2:]
    weight_in = jnp.where(moved, other_w[0], weight_in)
    weight_out = jnp.where(moved, other_w[1], weight_out)
    first_in = jnp.where(moved, other_m[0], first_in)
    second_in = jnp.where(moved, other_m[1], second_in)
    first_out = jnp.where(moved, other_m[2], first_out)
    second_out = jnp.where(moved, other_m[3], second_out)
    recv_x, recv_g = (
        lax.all_to_all(send_x, "expert", split_axis=0, concat_axis=0, tiled=True),
        lax.all_to_all(send_g, "expert", split_axis=0, concat_axis=0, tiled=True),
    )
    rows = recv_x.reshape(-1, width)
    grows = recv_g.reshape(-1, width)
    wb_in = weight_in.astype(jnp.bfloat16)
    wb_out = weight_out.astype(jnp.bfloat16)
    pre = jnp.dot(rows, wb_in, preferred_element_type=jnp.float32)
    hidden, pull = jax.vjp(gelu_tanh, pre)
    hidden = hidden.astype(jnp.bfloat16)
    part = jnp.dot(hidden, wb_out, preferred_element_type=jnp.float32).astype(jnp.bfloat16)
    dhid = lax.dot_general(
        grows, wb_out, (((1,), (1,)), ((), ())), preferred_element_type=jnp.float32
    )
    dpre = pull(dhid)[0].astype(jnp.bfloat16)
    xpart = lax.dot_general(
        dpre, wb_in, (((1,), (1,)), ((), ())), preferred_element_type=jnp.float32
    ).astype(jnp.bfloat16)
    grad_in = lax.dot_general(
        rows, dpre, (((0,), (0,)), ((), ())), preferred_element_type=jnp.float32
    )
    grad_out = lax.dot_general(
        hidden, grows, (((0,), (0,)), ((), ())), preferred_element_type=jnp.float32
    )
    back_part, back_dx = (
        lax.all_to_all(
            part.reshape(nexp, slots, width), "expert", split_axis=0, concat_axis=0, tiled=True
        ),
        lax.all_to_all(
            xpart.reshape(nexp, slots, width), "expert", split_axis=0, concat_axis=0, tiled=True
        ),
    )
    grad_in, grad_out = lax.psum((grad_in, grad_out), "dp")
    new_w_in, new_m_in, new_v_in = adamw(weight_in, first_in, second_in, grad_in)
    new_w_out, new_m_out, new_v_out = adamw(weight_out, first_out, second_out, grad_out)
    owns_pair = owns.astype(jnp.bfloat16)
    out_vals = jnp.dot(
        owns_pair, back_part.reshape(-1, width), preferred_element_type=jnp.float32
    )
    mixed = jnp.sum(out_vals.reshape(count, topk, width) * gates[:, :, None], axis=1).astype(
        jnp.bfloat16
    )
    token_grad = jnp.dot(
        owns_tok, back_dx.reshape(-1, width), preferred_element_type=jnp.float32
    ).astype(jnp.bfloat16)
    return (
        mixed,
        token_grad,
        new_w_in[None],
        new_w_out[None],
        new_m_in[None],
        new_v_in[None],
        new_m_out[None],
        new_v_out[None],
    )


def solution(mesh):
    in_specs = (
        P(("dp", "expert"), None),
        P(("dp", "expert"), None),
        P(("dp", "expert"), None),
        P(("dp", "expert"), None),
        P(),
        P(),
        P(),
        P("expert", None, None),
        P("expert", None, None),
        P("expert", None, None),
        P("expert", None, None),
        P("expert", None, None),
        P("expert", None, None),
    )
    out_specs = (
        P(("dp", "expert"), None),
        P(("dp", "expert"), None),
        P("expert", None, None),
        P("expert", None, None),
        P("expert", None, None),
        P("expert", None, None),
        P("expert", None, None),
        P("expert", None, None),
    )
    return jax.shard_map(body, mesh=mesh, in_specs=in_specs, out_specs=out_specs, check_vma=False)
```
